32 devices in a mesh: beam: 16 (over z, y, x), tp: 2 (over core).
Axes of the slice: x: 2, y: 2, z: 4, core: 2. Of those that a mesh axis runs over, the one named last changes fastest.
Arguments:
- head_input: bfloat16 [32, 8192], P('beam', 'tp'), may hold values from -6 to 6
- gate_input: bfloat16 [32, 8192], P('beam', 'tp'), may hold values from -6 to 6
- state_maps: bfloat16 [32, 2, 1024], P('beam'), may hold values from -6 to 6
- step_input: bfloat16 [32, 128], P('beam', 'tp'), may hold values from -4 to 4
- step_bias: float32 [128], P('tp'), may hold values from -4 to -1
- decay_log: float32 [128], P('tp'), may hold values from -1 to 2.5
- skip_gain: float32 [128], P('tp'), may hold values from 0.5 to 2
- norm_gain: float32 [8192], P('tp'), may hold values from 0.5 to 1.5
- recurrent_state: float32 [32, 128, 64, 256], P('beam', 'tp'), may hold values from -80 to 80
- queries: bfloat16 [32, 8192], P('beam', 'tp'), may hold values from -80 to 80
- fresh_cache: bfloat16 [32, 2, 1024], P('beam', None, 'tp'), may hold values from -6 to 6
- cache_pool: bfloat16 [320, 2, 64, 1024], P('beam', None, None, 'tp'), may hold values from -6 to 6
- page_table: int32 [32, 10], P('beam'), may hold values from 0 to 19, as said below
- context_length: int32 [32], replicated, may hold values from 64 to 640, as said below
- parents: int32 [32], replicated, may hold values from 0 to 31, as said below
Outputs:
- child_state: float32 [32, 128, 64, 256], P('beam', 'tp')
- mixer_out: bfloat16 [32, 8192], P('beam', 'tp')
- attention_out: bfloat16 [32, 8192], P('beam', 'tp')
The draws below stay inside these ranges and needn't reach their ends.
Inputs may be any that keep to these rules, and one draw needn't show every extreme that they name: `parents`: the parent of a child in block i of 2 beams lies in block i - 1, i or i + 1. In every block but the first exactly one child has its parent in the block below; in every block but the last exactly one has it in the block above; the others have theirs in their own block. `page_table`: in every block of 2 beams the rows name each of the block's 20 pages exactly once. `context_length`: some block of 2 beams has all lengths 640.
All inputs are finite; a program needn't handle non-finite values.
Results may differ from the reference program's by a relative error of at most 0.0035.
Values may be sent and summed in bfloat16 or wider, within the bound.
No kernel may reach another device: no remote copies, remote signals or barrier semaphores. Data moves between devices by JAX's collectives and lax.ppermute only.
A program may use at most 128 MiB of HBM per device.

```python
import jax
import jax.numpy as jnp
from jax import lax

BEAMS_DEV = 2
PAGES = 10
PAGE = 64
HEADS = 128
HEAD_DIM = 64
STATE = 256
GROUPS = 4
QHEADS = 64
KVHEADS = 8
ATT_DIM = 128
BEAMS = 32
CONTEXT = 640
POOL_DEV = 20
POOL = 320


def draw_recurrent_state(key, part):
    first, second = jax.random.split(jax.random.fold_in(key, 11), 2)
    head_scale = jnp.exp(jax.random.uniform(first, (1, HEADS, 1, 1), jnp.float32, -1.15, 1.15))
    base = jnp.clip(jax.random.normal(second, (BEAMS, HEADS, HEAD_DIM, STATE), jnp.float32), -6.0, 6.0)
    return (base * head_scale).astype(jnp.float32)


def draw_queries(key, part):
    first = jax.random.fold_in(jax.random.fold_in(key, 23), 0)
    values = jnp.clip(jax.random.normal(first, (BEAMS, QHEADS, ATT_DIM), jnp.float32), -6.0, 6.0)
    return values.reshape(BEAMS, QHEADS * ATT_DIM).astype(jnp.bfloat16)


def draw_cache_pool(key, part):
    first = jax.random.fold_in(key, 37)
    values = jnp.clip(jax.random.normal(first, (POOL, 2, PAGE, KVHEADS * ATT_DIM), jnp.float32), -6.0, 6.0)
    return values.astype(jnp.bfloat16)


def draw_page_table(key, part):
    blocks = BEAMS // BEAMS_DEV
    keys_all = jax.random.split(jax.random.fold_in(key, 41), blocks)
    orders = jax.vmap(lambda single: jax.random.permutation(single, POOL_DEV))(keys_all)
    return orders.reshape(BEAMS, PAGES).astype(jnp.int32)


def draw_context_length(key, part):
    first, second = jax.random.split(jax.random.fold_in(key, 53))
    base = jax.random.randint(first, (BEAMS,), PAGE, CONTEXT + 1)
    filled = jax.random.randint(second, (), 0, BEAMS // BEAMS_DEV)
    blocks = jnp.arange(BEAMS) // BEAMS_DEV
    return jnp.where(blocks == filled, CONTEXT, base).astype(jnp.int32)


def draw_parents(key, part):
    blocks = BEAMS // BEAMS_DEV
    ka, kb, kc, kd, ke = jax.random.split(jax.random.fold_in(key, 67), 5)
    leader = jax.random.randint(ka, (blocks,), 0, BEAMS_DEV)
    below_slot = jax.random.randint(kb, (blocks,), 0, BEAMS_DEV)
    above_slot = (below_slot + jax.random.randint(kc, (blocks,), 1, BEAMS_DEV)) % BEAMS_DEV
    block_ids = jnp.arange(blocks)[:, None]
    slots = jnp.arange(BEAMS_DEV)[None, :]
    offset = jnp.where((slots == below_slot[:, None]) & (block_ids > 0), -1, 0)
    offset = jnp.where((slots == above_slot[:, None]) & (block_ids < blocks - 1), 1, offset)
    source = block_ids + offset
    follow = jax.random.randint(kd, (blocks, BEAMS_DEV), 0, 2) == 0
    anywhere = jax.random.randint(ke, (blocks, BEAMS_DEV), 0, BEAMS_DEV)
    pick = jnp.where(follow, leader[source], anywhere)
    first_slot = (above_slot[0] + 1) % BEAMS_DEV
    last_slot = (below_slot[blocks - 1] + 1) % BEAMS_DEV
    pick = jnp.where((block_ids == 0) & (slots == first_slot), 0, pick)
    pick = jnp.where((block_ids == blocks - 1) & (slots == last_slot), BEAMS_DEV - 1, pick)
    return (source * BEAMS_DEV + pick).reshape(BEAMS).astype(jnp.int32)


def level_of(key, shape, cuts, least, largest):
    def one(position, shards_of):
        draws = jax.random.uniform(jax.random.fold_in(jax.random.fold_in(key, 6), position), (shards_of,), jnp.float32, least / len(cuts), largest / len(cuts))
        return jnp.repeat(jnp.exp(draws), shape[position] // shards_of).reshape((-1,) + (1,) * (len(shape) - position - 1))

    loudness = one(*cuts[0])
    for cut in cuts[1:]:
        loudness = loudness * one(*cut)
    return loudness


def normal_values(own_key, dims, width, most, cuts=(), kind=jnp.bfloat16):
    factor_of = level_of(own_key, dims, cuts, -0.22, 0.18) if cuts else 1.0
    values = jax.random.normal(own_key, dims, jnp.float32) * width * factor_of
    return jnp.minimum(jnp.maximum(values, -most), most).astype(kind)


def setup_inputs(seed: int = 0) -> dict:
    streams_of = jax.random.split(jax.random.key(seed), 16)
    return {
        "head_input": normal_values(streams_of[0], (BEAMS, HEADS * HEAD_DIM), 1.0, 6.0, ((0, 16), (1, 2))),
        "gate_input": normal_values(streams_of[1], (BEAMS, HEADS * HEAD_DIM), 1.0, 6.0, ((0, 16), (1, 2))),
        "state_maps": normal_values(streams_of[2], (BEAMS, 2, GROUPS * STATE), 1.0, 6.0, ((0, 16),)),
        "step_input": normal_values(streams_of[3], (BEAMS, HEADS), 1.0, 4.0, ((0, 16), (1, 2))),
        "step_bias": jnp.clip(-4.0 + 3.0 * jax.random.uniform(streams_of[4], (HEADS,), jnp.float32) ** level_of(streams_of[4], (HEADS,), ((0, 2),), -0.2, 0.2), -4.0, -1.0),
        "decay_log": jnp.clip(-1.0 + 3.5 * jax.random.uniform(streams_of[5], (HEADS,), jnp.float32) ** level_of(streams_of[5], (HEADS,), ((0, 2),), -0.2, 0.2), -1.0, 2.5),
        "skip_gain": jnp.clip(0.5 + 1.5 * jax.random.uniform(streams_of[6], (HEADS,), jnp.float32) ** level_of(streams_of[6], (HEADS,), ((0, 2),), -0.2, 0.2), 0.5, 2.0),
        "norm_gain": jnp.clip(1.0 + 0.1 * jax.random.normal(streams_of[7], (HEADS * HEAD_DIM,), jnp.float32), 0.5, 1.5),
        "recurrent_state": draw_recurrent_state(jax.random.fold_in(streams_of[15], 71), 0),
        "queries": draw_queries(jax.random.fold_in(streams_of[15], 71), 0),
        "fresh_cache": normal_values(streams_of[10], (BEAMS, 2, KVHEADS * ATT_DIM), 1.0, 6.0, ((0, 16), (2, 2))),
        "cache_pool": draw_cache_pool(jax.random.fold_in(streams_of[15], 71), 0),
        "page_table": draw_page_table(jax.random.fold_in(streams_of[15], 71), 0),
        "context_length": draw_context_length(jax.random.fold_in(streams_of[15], 71), 0),
        "parents": draw_parents(jax.random.fold_in(streams_of[15], 71), 0),
    }


def reference(head_input, gate_input, state_maps, step_input, step_bias, decay_log, skip_gain, norm_gain, recurrent_state, queries, fresh_cache, cache_pool, page_table, context_length, parents):
    per_group = HEADS // GROUPS
    inputs_x = head_input.astype(jnp.float32).reshape(BEAMS, HEADS, HEAD_DIM)
    gate_values = gate_input.astype(jnp.float32).reshape(BEAMS, HEADS, HEAD_DIM)
    maps_all = state_maps.astype(jnp.float32).reshape(BEAMS, 2, GROUPS, STATE)
    input_maps = jnp.tile(maps_all[:, 0], (1, per_group, 1))
    output_maps = jnp.tile(maps_all[:, 1], (1, per_group, 1))
    step_size = jax.nn.softplus(step_input.astype(jnp.float32) + step_bias)
    retain = jnp.exp(-step_size * jnp.exp(decay_log))

    def fork(child):
        parent = parents[child]
        carried = recurrent_state[parent]
        updated = retain[child][:, None, None] * carried + (step_size[child][:, None] * inputs_x[child])[:, :, None] * input_maps[child][:, None, :]
        mixed = lax.optimization_barrier(jnp.sum(updated * output_maps[child][:, None, :], axis=-1)) + skip_gain[:, None] * inputs_x[child]
        return (updated, mixed)
    child_state, mixed_all = lax.map(fork, jnp.arange(BEAMS, dtype=jnp.int32))
    gated_out = mixed_all * jax.nn.silu(gate_values)
    grouped = gated_out.reshape(BEAMS, per_group, GROUPS, HEAD_DIM)
    inverse = lax.rsqrt(lax.optimization_barrier(jnp.sum(grouped * grouped, axis=(1, 3))) / (per_group * HEAD_DIM) + 1e-05)
    mixer_out = ((grouped * inverse[:, None, :, None]).reshape(BEAMS, HEADS * HEAD_DIM) * norm_gain).astype(jnp.bfloat16)
    query_group = QHEADS // KVHEADS
    factor = ATT_DIM ** (-0.5)

    def attend(child):
        parent = parents[child]
        home = parent // BEAMS_DEV
        pages = (page_table[parent] + home * POOL_DEV).astype(jnp.int32)
        block = cache_pool[pages]
        key_rows = block[:, 0].reshape(CONTEXT, KVHEADS, ATT_DIM).astype(jnp.float32)
        value_rows = block[:, 1].reshape(CONTEXT, KVHEADS, ATT_DIM).astype(jnp.float32)
        query_rows = queries[child].astype(jnp.float32).reshape(KVHEADS, query_group, ATT_DIM)
        fresh_key = fresh_cache[child, 0].astype(jnp.float32).reshape(KVHEADS, ATT_DIM)
        fresh_value = fresh_cache[child, 1].astype(jnp.float32).reshape(KVHEADS, ATT_DIM)
        scores = jnp.einsum('gqd,tgd->gqt', query_rows, key_rows) * factor
        own_score = jnp.einsum('gqd,gd->gq', query_rows, fresh_key) * factor
        live_mask = (jnp.arange(CONTEXT, dtype=jnp.int32) < context_length[parent])[None, None, :]
        masked = jnp.where(live_mask, scores, -1e+30)
        highest = jnp.maximum(lax.optimization_barrier(jnp.max(masked, axis=-1)), own_score)
        raw_weights = jnp.where(live_mask, jnp.exp(masked - highest[..., None]), 0.0)
        weights = lax.optimization_barrier(raw_weights.astype(jnp.bfloat16)).astype(jnp.float32)
        own_weight = lax.optimization_barrier(jnp.exp(own_score - highest).astype(jnp.bfloat16)).astype(jnp.float32)
        denom = lax.optimization_barrier(jnp.sum(weights, axis=-1)) + own_weight
        numer = jnp.einsum('gqt,tgd->gqd', weights, value_rows) + own_weight[..., None] * fresh_value[:, None, :]
        return (numer / denom[..., None]).reshape(QHEADS * ATT_DIM).astype(jnp.bfloat16)
    attention_out = lax.map(attend, jnp.arange(BEAMS, dtype=jnp.int32))
    return (child_state, mixer_out, attention_out)
```

```python
import functools

import jax
import jax.numpy as jnp
from jax import lax
from jax.experimental import pallas as pl
from jax.experimental.pallas import tpu as pltpu
from jax.sharding import PartitionSpec as P

HEADS = 128
GROUPS = 4
ATT_DIM = 128
CHUNK_EIGHTHS = (2, 3, 2, 1)


def from_behind(value, axis, steps):
    count = lax.axis_size(axis)
    leading, last = (max(0, -steps), min(count, count - steps))
    return lax.ppermute(value, axis, [(source, source + steps) for source in range(leading, last)])


def narrow_kernel(picks_ref, state_up, state_down, up_ref, down_ref):
    up_ref[...] = state_up[0].astype(jnp.bfloat16)
    down_ref[...] = state_down[0].astype(jnp.bfloat16)


def narrow(state, picks, first, count, block):
    _, _, head_dim, state_dim = state.shape
    base = first // block
    out = jax.ShapeDtypeStruct((count, head_dim, state_dim), jnp.bfloat16)
    out_spec = pl.BlockSpec((block, head_dim, state_dim), lambda i, picks: (i, 0, 0))
    return pl.pallas_call(
        narrow_kernel,
        out_shape=(out, out),
        grid_spec=pltpu.PrefetchScalarGridSpec(
            num_scalar_prefetch=1,
            grid=(count // block,),
            in_specs=[
                pl.BlockSpec(
                    (1, block, head_dim, state_dim), lambda i, picks: (picks[0], base + i, 0, 0)
                ),
                pl.BlockSpec(
                    (1, block, head_dim, state_dim), lambda i, picks: (picks[1], base + i, 0, 0)
                ),
            ],
            out_specs=(out_spec, out_spec),
        ),
        cost_estimate=pl.CostEstimate(
            flops=0, bytes_accessed=12 * count * head_dim * state_dim, transcendentals=0
        ),
        name="narrow",
    )(picks, state, state)


def grow_kernel(base, block, relative, local, own, below, above, drive, retain, maps, *rest):
    out = rest[-1]
    child = pl.program_id(0)
    head = (base + pl.program_id(1)) * block
    where_from = relative[child]

    def update(previous):
        for j in range(block):
            out[0, j] = (
                retain[child, head + j] * previous(j)
                + drive[0, 0, :, j : j + 1] * maps[0, j % GROUPS : j % GROUPS + 1]
            )

    @pl.when(where_from == 0)
    def _():
        update(lambda j: own[0, j])

    @pl.when(where_from < 0)
    def _():
        update(lambda j: below[j].astype(jnp.float32))

    @pl.when(where_from > 0)
    def _():
        update(lambda j: above[j].astype(jnp.float32))


def grow(relative, local, state, below, above, drive, retain, maps, first, block, partial):
    beams, _, head_dim, state_dim = state.shape
    count = below.shape[0]
    base = first // block

    def own_map(c, i, relative, local):
        mine = relative[c] == 0
        return (jnp.where(mine, local[c], 0), jnp.where(mine, base + i, base), 0, 0)

    def below_map(c, i, relative, local):
        return (jnp.where(relative[c] < 0, i, 0), 0, 0)

    def above_map(c, i, relative, local):
        return (jnp.where(relative[c] > 0, i, 0), 0, 0)

    in_specs = [
        pl.BlockSpec((1, block, head_dim, state_dim), own_map),
        pl.BlockSpec((block, head_dim, state_dim), below_map),
        pl.BlockSpec((block, head_dim, state_dim), above_map),
        pl.BlockSpec((1, 1, head_dim, block), lambda c, i, *_: (c, base + i, 0, 0)),
        pl.BlockSpec(memory_space=pltpu.SMEM),
        pl.BlockSpec((1, GROUPS, state_dim), lambda c, i, *_: (c, 0, 0)),
    ]
    operands = [state, below, above, drive, retain, maps]
    aliases = {}
    if partial is not None:
        in_specs.append(pl.BlockSpec(memory_space=pl.ANY))
        operands.append(partial)
        aliases = {8: 0}
    return pl.pallas_call(
        functools.partial(grow_kernel, base, block),
        out_shape=jax.ShapeDtypeStruct(state.shape, jnp.float32),
        grid_spec=pltpu.PrefetchScalarGridSpec(
            num_scalar_prefetch=2,
            grid=(beams, count // block),
            in_specs=in_specs,
            out_specs=pl.BlockSpec(
                (1, block, head_dim, state_dim), lambda c, i, *_: (c, base + i, 0, 0)
            ),
        ),
        input_output_aliases=aliases,
        cost_estimate=pl.CostEstimate(
            flops=4 * beams * count * head_dim * state_dim,
            bytes_accessed=6 * beams * count * head_dim * state_dim,
            transcendentals=0,
        ),
        name="grow",
    )(relative, local, *operands)


def attend_kernel(table, lengths, query, fresh, pool, out, pages, sems):
    count, page_count = table.shape
    kv_heads = query.shape[1]
    positions = page_count * pool.shape[2]
    factor = ATT_DIM ** (-0.5)
    copies = [
        [
            pltpu.make_async_copy(pool.at[table[c, j]], pages.at[c, j], sems.at[c, j])
            for j in range(page_count)
        ]
        for c in range(count)
    ]
    for group in copies:
        for copy in group:
            copy.start()
    for c in range(count):
        for copy in copies[c]:
            copy.wait()
        length = lengths[c]
        for g in range(kv_heads):
            lanes = slice(g * ATT_DIM, (g + 1) * ATT_DIM)
            rows = query[c, g]
            keys = pages[c, :, 0, :, lanes].reshape(positions, ATT_DIM)
            values = pages[c, :, 1, :, lanes].reshape(positions, ATT_DIM)
            own_key = fresh[c, 0, g : g + 1].astype(jnp.float32)
            own_value = fresh[c, 1, g : g + 1].astype(jnp.float32)
            scores = (
                lax.dot_general(
                    rows, keys, (((1,), (1,)), ((), ())), preferred_element_type=jnp.float32
                )
                * factor
            )
            own_score = (
                jnp.sum(rows.astype(jnp.float32) * own_key, axis=1, keepdims=True) * factor
            )
            live = lax.broadcasted_iota(jnp.int32, scores.shape, 1) < length
            masked = jnp.where(live, scores, -1e30)
            highest = jnp.maximum(jnp.max(masked, axis=1, keepdims=True), own_score)
            weights = jnp.where(live, jnp.exp(masked - highest), 0.0).astype(jnp.bfloat16)
            own_weight = jnp.exp(own_score - highest).astype(jnp.bfloat16).astype(jnp.float32)
            total = jnp.sum(weights.astype(jnp.float32), axis=1, keepdims=True) + own_weight
            summed = jnp.dot(weights, values, preferred_element_type=jnp.float32)
            out[c, g] = (summed + own_weight * own_value) / total


def attend(table, lengths, query, fresh, pool):
    count, page_count = table.shape
    vmem = pl.BlockSpec(memory_space=pltpu.VMEM)
    smem = pl.BlockSpec(memory_space=pltpu.SMEM)
    return pl.pallas_call(
        attend_kernel,
        out_shape=jax.ShapeDtypeStruct(query.shape, jnp.float32),
        in_specs=[smem, smem, vmem, vmem, pl.BlockSpec(memory_space=pl.ANY)],
        out_specs=vmem,
        scratch_shapes=[
            pltpu.VMEM((count, page_count) + pool.shape[1:], jnp.bfloat16),
            pltpu.SemaphoreType.DMA((count, page_count)),
        ],
        cost_estimate=pl.CostEstimate(
            flops=4 * query.size * page_count * pool.shape[2],
            bytes_accessed=2 * count * page_count * pool.size // pool.shape[0],
            transcendentals=query.size * page_count * pool.shape[2] // ATT_DIM,
        ),
        name="attend",
    )(table, lengths, query, fresh, pool)


def shards(
    head_input,
    gate_input,
    state_maps,
    step_input,
    step_bias,
    decay_log,
    skip_gain,
    norm_gain,
    recurrent_state,
    queries,
    fresh_cache,
    cache_pool,
    page_table,
    context_length,
    parents,
):
    local_beams, local_heads, head_dim, state_dim = recurrent_state.shape
    total_beams = parents.shape[0]
    query_width = queries.shape[1]
    kv_width = fresh_cache.shape[2]
    kv_heads = kv_width // ATT_DIM
    map_width = state_maps.shape[2]
    block = min(8, local_heads // 8)
    block = max(block, GROUPS) if local_heads % GROUPS == 0 else block
    device = lax.axis_index("beam")
    slots = jnp.arange(local_beams, dtype=jnp.int32)
    own_parents = lax.dynamic_slice_in_dim(parents, device * local_beams, local_beams)
    source = own_parents // local_beams
    relative = (source - device).astype(jnp.int32)
    local_index = jnp.clip(own_parents - source * local_beams, 0, local_beams - 1)

    def wanted_by(direction):
        start = jnp.clip((device + direction) * local_beams, 0, total_beams - local_beams)
        theirs = lax.dynamic_slice_in_dim(parents, start, local_beams)
        found = theirs // local_beams == device
        index = jnp.sum(jnp.where(found, theirs - device * local_beams, 0))
        return jnp.clip(index, 0, local_beams - 1).astype(jnp.int32)

    wanted_above = wanted_by(1)
    wanted_below = wanted_by(-1)
    slot_above = jnp.sum(jnp.where(relative > 0, slots, 0))
    slot_below = jnp.sum(jnp.where(relative < 0, slots, 0))

    picks = jnp.stack([wanted_above, wanted_below])
    unit = local_heads // 8
    sizes = [eighths * unit for eighths in CHUNK_EIGHTHS]
    if unit % GROUPS:
        sizes = [local_heads // 2, local_heads // 2]
    firsts = [sum(sizes[:k]) for k in range(len(sizes))]
    arrived = []
    for first, size in zip(firsts, sizes):
        up, down = narrow(recurrent_state, picks, first, size, block)
        arrived.append((from_behind(up, "beam", 1), from_behind(down, "beam", -1)))

    asked = jnp.concatenate(
        [queries, fresh_cache.reshape(local_beams, 2 * kv_width), state_maps[:, 1]], axis=1
    )
    ask_above = lax.dynamic_index_in_dim(asked, slot_above, 0, keepdims=False)
    ask_below = lax.dynamic_index_in_dim(asked, slot_below, 0, keepdims=False)
    from_below = from_behind(ask_above, "beam", 1)
    from_above = from_behind(ask_below, "beam", -1)

    def by_origin(own, below, above):
        shape = (-1,) + (1,) * (own.ndim - 1)
        picked = jnp.where((relative < 0).reshape(shape), below[None], above[None])
        return jnp.where((relative == 0).reshape(shape), own, picked)

    served = by_origin(asked, from_below, from_above)
    served_parent = jnp.where(
        relative == 0, local_index, jnp.where(relative < 0, wanted_below, wanted_above)
    ).astype(jnp.int32)
    served_query = served[:, :query_width].reshape(local_beams, kv_heads, -1, ATT_DIM)
    served_fresh = served[:, query_width : query_width + 2 * kv_width].reshape(
        local_beams, 2, kv_heads, ATT_DIM
    )
    served_maps = (
        served[:, query_width + 2 * kv_width :]
        .reshape(local_beams, GROUPS, state_dim)
        .astype(jnp.float32)
    )
    table = jnp.take(page_table, served_parent, axis=0)
    lengths = jnp.take(context_length, device * local_beams + served_parent)
    attended = attend(table, lengths, served_query, served_fresh, cache_pool)
    read_out = []
    for c in range(local_beams):
        parent_state = lax.dynamic_index_in_dim(
            recurrent_state, served_parent[c], 0, keepdims=False
        ).reshape(local_heads // GROUPS, GROUPS, head_dim, state_dim)
        read_out.append(
            jnp.sum(parent_state * served_maps[c][None, :, None, :], axis=-1).reshape(-1)
        )
    replies = jnp.concatenate([attended.reshape(local_beams, -1), jnp.stack(read_out)], axis=1)
    reply_above = lax.dynamic_index_in_dim(replies, slot_above, 0, keepdims=False)
    reply_below = lax.dynamic_index_in_dim(replies, slot_below, 0, keepdims=False)
    reply_from_below = from_behind(reply_above, "beam", 1)
    reply_from_above = from_behind(reply_below, "beam", -1)
    answer = by_origin(replies, reply_from_below, reply_from_above)
    attention_out = answer[:, :query_width].astype(jnp.bfloat16)

    inputs_x = head_input.astype(jnp.float32).reshape(local_beams, local_heads, head_dim)
    gate_values = gate_input.astype(jnp.float32).reshape(local_beams, local_heads, head_dim)
    step_size = jax.nn.softplus(step_input.astype(jnp.float32) + step_bias)
    retain = jnp.exp(-step_size * jnp.exp(decay_log))
    maps_all = state_maps.astype(jnp.float32).reshape(local_beams, 2, GROUPS, state_dim)
    drive = step_size[:, :, None] * inputs_x

    per_group = HEADS // GROUPS
    rows = local_heads // GROUPS
    overlap = jnp.sum(maps_all[:, 0] * maps_all[:, 1], axis=-1)
    overlap_heads = jnp.tile(overlap, (1, rows))
    read_back = answer[:, query_width:].reshape(local_beams, local_heads, head_dim)
    mixed_all = (
        retain[:, :, None] * read_back
        + drive * overlap_heads[:, :, None]
        + skip_gain[None, :, None] * inputs_x
    )
    gated_out = mixed_all * jax.nn.silu(gate_values)
    head_power = jnp.sum(gated_out * gated_out, axis=-1)
    partial_power = jnp.sum(head_power.reshape(local_beams, rows, GROUPS), axis=1)
    group_power = lax.psum(partial_power, "tp")
    inverse = lax.rsqrt(group_power / (per_group * head_dim) + 1e-05)
    inverse_heads = jnp.tile(inverse, (1, rows))
    mixer_out = (
        (gated_out * inverse_heads[..., None]).reshape(local_beams, local_heads * head_dim)
        * norm_gain
    ).astype(jnp.bfloat16)

    drive_columns = drive.reshape(local_beams, local_heads // block, block, head_dim).transpose(
        0, 1, 3, 2
    )
    child_state = None
    for first, (below, above) in zip(firsts, arrived):
        child_state = grow(
            relative,
            local_index,
            recurrent_state,
            below,
            above,
            drive_columns,
            retain,
            maps_all[:, 0],
            first,
            block,
            child_state,
        )
    return (child_state, mixer_out, attention_out)


def solution(mesh):
    return jax.shard_map(
        shards,
        mesh=mesh,
        in_specs=(
            P("beam", "tp"),
            P("beam", "tp"),
            P("beam", None, None),
            P("beam", "tp"),
            P("tp"),
            P("tp"),
            P("tp"),
            P("tp"),
            P("beam", "tp", None, None),
            P("beam", "tp"),
            P("beam", None, "tp"),
            P("beam", None, None, "tp"),
            P("beam", None),
            P(),
            P(),
        ),
        out_specs=(P("beam", "tp", None, None), P("beam", "tp"), P("beam", "tp")),
        check_vma=False,
    )
```

```python
import functools

import jax
import jax.numpy as jnp
from jax import lax
from jax.experimental import pallas as pl
from jax.experimental.pallas import tpu as pltpu
from jax.sharding import PartitionSpec as P


HEADS = 128
GROUPS = 4
ATT_DIM = 128
CHUNK_EIGHTHS = (2, 3, 2, 1)


def from_behind(value, axis, steps):
    count = lax.axis_size(axis)
    leading, last = (max(0, -steps), min(count, count - steps))
    return lax.ppermute(value, axis, [(source, source + steps) for source in range(leading, last)])


def wanted_by(parents, device, direction, local_beams, total_beams):
    start = jnp.clip((device + direction) * local_beams, 0, total_beams - local_beams)
    index = jnp.int32(0)
    for j in range(local_beams):
        offset = parents[start + j] - device * local_beams
        index = jnp.where((offset >= 0) & (offset < local_beams), offset, index)
    return index


def narrow_kernel(parents, device, state_up, state_down, up_ref, down_ref):
    up_ref[...] = state_up[0].astype(jnp.bfloat16)
    down_ref[...] = state_down[0].astype(jnp.bfloat16)


def narrow(state, parents, device, first, count, block):
    local_beams, _, head_dim, state_dim = state.shape
    total_beams = parents.shape[0]
    base = first // block
    out = jax.ShapeDtypeStruct((count, head_dim, state_dim), jnp.bfloat16)
    out_spec = pl.BlockSpec((block, head_dim, state_dim), lambda i, *_: (i, 0, 0))

    def state_spec(direction):
        def index(i, parents, device):
            pick = wanted_by(parents, device[0], direction, local_beams, total_beams)
            return (pick, base + i, 0, 0)

        return pl.BlockSpec((1, block, head_dim, state_dim), index)

    return pl.pallas_call(
        narrow_kernel,
        out_shape=(out, out),
        grid_spec=pltpu.PrefetchScalarGridSpec(
            num_scalar_prefetch=2,
            grid=(count // block,),
            in_specs=[state_spec(1), state_spec(-1)],
            out_specs=(out_spec, out_spec),
        ),
        cost_estimate=pl.CostEstimate(
            flops=0, bytes_accessed=12 * count * head_dim * state_dim, transcendentals=0
        ),
        compiler_params=pltpu.CompilerParams(vmem_limit_bytes=60 * 2**20),
        name="narrow",
    )(parents, device, state, state)


def grow_kernel(base, block, relative, local, own, below, above, drive, retain, maps, *rest):
    out = rest[-1]
    child = pl.program_id(0)
    head = (base + pl.program_id(1)) * block
    where_from = relative[child]

    def update(previous):
        for j in range(block):
            out[0, j] = (
                retain[child, head + j] * previous(j)
                + drive[0, 0, :, j : j + 1] * maps[0, j % GROUPS : j % GROUPS + 1]
            )

    @pl.when(where_from == 0)
    def _():
        update(lambda j: own[0, j])

    @pl.when(where_from < 0)
    def _():
        update(lambda j: below[j].astype(jnp.float32))

    @pl.when(where_from > 0)
    def _():
        update(lambda j: above[j].astype(jnp.float32))


def grow(relative, local, state, below, above, drive, retain, maps, first, block, partial):
    beams, _, head_dim, state_dim = state.shape
    count = below.shape[0]
    base = first // block

    def own_map(c, i, relative, local):
        mine = relative[c] == 0
        return (jnp.where(mine, local[c], 0), jnp.where(mine, base + i, base), 0, 0)

    def below_map(c, i, relative, local):
        return (jnp.where(relative[c] < 0, i, 0), 0, 0)

    def above_map(c, i, relative, local):
        return (jnp.where(relative[c] > 0, i, 0), 0, 0)

    in_specs = [
        pl.BlockSpec((1, block, head_dim, state_dim), own_map),
        pl.BlockSpec((block, head_dim, state_dim), below_map),
        pl.BlockSpec((block, head_dim, state_dim), above_map),
        pl.BlockSpec((1, 1, head_dim, block), lambda c, i, *_: (c, base + i, 0, 0)),
        pl.BlockSpec(memory_space=pltpu.SMEM),
        pl.BlockSpec((1, GROUPS, state_dim), lambda c, i, *_: (c, 0, 0)),
    ]
    operands = [state, below, above, drive, retain, maps]
    aliases = {}
    if partial is not None:
        in_specs.append(pl.BlockSpec(memory_space=pl.ANY))
        operands.append(partial)
        aliases = {8: 0}
    return pl.pallas_call(
        functools.partial(grow_kernel, base, block),
        out_shape=jax.ShapeDtypeStruct(state.shape, jnp.float32),
        grid_spec=pltpu.PrefetchScalarGridSpec(
            num_scalar_prefetch=2,
            grid=(beams, count // block),
            in_specs=in_specs,
            out_specs=pl.BlockSpec(
                (1, block, head_dim, state_dim), lambda c, i, *_: (c, base + i, 0, 0)
            ),
        ),
        input_output_aliases=aliases,
        cost_estimate=pl.CostEstimate(
            flops=4 * beams * count * head_dim * state_dim,
            bytes_accessed=6 * beams * count * head_dim * state_dim,
            transcendentals=0,
        ),
        compiler_params=pltpu.CompilerParams(vmem_limit_bytes=60 * 2**20),
        name="grow",
    )(relative, local, *operands)


def attend_kernel(table, lengths, query, fresh, pool, out, pages, sems):
    count, page_count = table.shape
    kv_heads = query.shape[1]
    positions = page_count * pool.shape[2]
    factor = ATT_DIM ** (-0.5)
    copies = [
        [
            pltpu.make_async_copy(pool.at[table[c, j]], pages.at[c, j], sems.at[c, j])
            for j in range(page_count)
        ]
        for c in range(count)
    ]
    for group in copies:
        for copy in group:
            copy.start()
    for c in range(count):
        for copy in copies[c]:
            copy.wait()
        length = lengths[c]
        for g in range(kv_heads):
            lanes = slice(g * ATT_DIM, (g + 1) * ATT_DIM)
            rows = query[c, g]
            keys = pages[c, :, 0, :, lanes].reshape(positions, ATT_DIM)
            values = pages[c, :, 1, :, lanes].reshape(positions, ATT_DIM)
            own_key = fresh[c, 0, g : g + 1].astype(jnp.float32)
            own_value = fresh[c, 1, g : g + 1].astype(jnp.float32)
            scores = (
                lax.dot_general(
                    rows, keys, (((1,), (1,)), ((), ())), preferred_element_type=jnp.float32
                )
                * factor
            )
            own_score = (
                jnp.sum(rows.astype(jnp.float32) * own_key, axis=1, keepdims=True) * factor
            )
            live = lax.broadcasted_iota(jnp.int32, scores.shape, 1) < length
            masked = jnp.where(live, scores, -1e30)
            highest = jnp.maximum(jnp.max(masked, axis=1, keepdims=True), own_score)
            weights = jnp.where(live, jnp.exp(masked - highest), 0.0).astype(jnp.bfloat16)
            own_weight = jnp.exp(own_score - highest).astype(jnp.bfloat16).astype(jnp.float32)
            total = jnp.sum(weights.astype(jnp.float32), axis=1, keepdims=True) + own_weight
            summed = jnp.dot(weights, values, preferred_element_type=jnp.float32)
            out[c, g] = (summed + own_weight * own_value) / total


def attend(table, lengths, query, fresh, pool):
    count, page_count = table.shape
    vmem = pl.BlockSpec(memory_space=pltpu.VMEM)
    smem = pl.BlockSpec(memory_space=pltpu.SMEM)
    return pl.pallas_call(
        attend_kernel,
        out_shape=jax.ShapeDtypeStruct(query.shape, jnp.float32),
        in_specs=[smem, smem, vmem, vmem, pl.BlockSpec(memory_space=pl.ANY)],
        out_specs=vmem,
        scratch_shapes=[
            pltpu.VMEM((count, page_count) + pool.shape[1:], jnp.bfloat16),
            pltpu.SemaphoreType.DMA((count, page_count)),
        ],
        cost_estimate=pl.CostEstimate(
            flops=4 * query.size * page_count * pool.shape[2],
            bytes_accessed=2 * count * page_count * pool.size // pool.shape[0],
            transcendentals=query.size * page_count * pool.shape[2] // ATT_DIM,
        ),
        name="attend",
    )(table, lengths, query, fresh, pool)


def shards(
    head_input,
    gate_input,
    state_maps,
    step_input,
    step_bias,
    decay_log,
    skip_gain,
    norm_gain,
    recurrent_state,
    queries,
    fresh_cache,
    cache_pool,
    page_table,
    context_length,
    parents,
):
    local_beams, local_heads, head_dim, state_dim = recurrent_state.shape
    total_beams = parents.shape[0]
    query_width = queries.shape[1]
    kv_width = fresh_cache.shape[2]
    kv_heads = kv_width // ATT_DIM
    block = min(8, local_heads // 8)
    block = max(block, GROUPS) if local_heads % GROUPS == 0 else block
    device = lax.axis_index("beam")
    slots = jnp.arange(local_beams, dtype=jnp.int32)
    own_parents = lax.dynamic_slice_in_dim(parents, device * local_beams, local_beams)
    source = own_parents // local_beams
    relative = (source - device).astype(jnp.int32)
    local_index = jnp.clip(own_parents - source * local_beams, 0, local_beams - 1)

    wanted_above = wanted_by(parents, device, 1, local_beams, total_beams)
    wanted_below = wanted_by(parents, device, -1, local_beams, total_beams)
    slot_above = jnp.sum(jnp.where(relative > 0, slots, 0))
    slot_below = jnp.sum(jnp.where(relative < 0, slots, 0))

    place = device.reshape(1).astype(jnp.int32)
    unit = local_heads // 8
    sizes = [eighths * unit for eighths in CHUNK_EIGHTHS]
    if unit % GROUPS:
        sizes = [local_heads // 2, local_heads // 2]
    firsts = [sum(sizes[:k]) for k in range(len(sizes))]
    arrived = []
    for first, size in zip(firsts, sizes):
        up, down = narrow(recurrent_state, parents, place, first, size, block)
        below = from_behind(up, "beam", 1)
        above = from_behind(down, "beam", -1)
        arrived.append((below, above))

    asked = jnp.concatenate(
        [queries, fresh_cache.reshape(local_beams, 2 * kv_width), state_maps[:, 1]], axis=1
    )
    ask_above = lax.dynamic_index_in_dim(asked, slot_above, 0, keepdims=False)
    ask_below = lax.dynamic_index_in_dim(asked, slot_below, 0, keepdims=False)
    from_below = from_behind(ask_above, "beam", 1)
    from_above = from_behind(ask_below, "beam", -1)

    def by_origin(own, below, above):
        shape = (-1,) + (1,) * (own.ndim - 1)
        picked = jnp.where((relative < 0).reshape(shape), below[None], above[None])
        return jnp.where((relative == 0).reshape(shape), own, picked)

    served = by_origin(asked, from_below, from_above)
    served_parent = jnp.where(
        relative == 0, local_index, jnp.where(relative < 0, wanted_below, wanted_above)
    ).astype(jnp.int32)
    served_query = served[:, :query_width].reshape(local_beams, kv_heads, -1, ATT_DIM)
    served_fresh = served[:, query_width : query_width + 2 * kv_width].reshape(
        local_beams, 2, kv_heads, ATT_DIM
    )
    served_maps = (
        served[:, query_width + 2 * kv_width :]
        .reshape(local_beams, GROUPS, state_dim)
        .astype(jnp.float32)
    )
    table = jnp.take(page_table, served_parent, axis=0)
    lengths = jnp.take(context_length, device * local_beams + served_parent)
    attended = attend(table, lengths, served_query, served_fresh, cache_pool)
    read_out = []
    for c in range(local_beams):
        parent_state = lax.dynamic_index_in_dim(
            recurrent_state, served_parent[c], 0, keepdims=False
        ).reshape(local_heads // GROUPS, GROUPS, head_dim, state_dim)
        read_out.append(
            jnp.sum(parent_state * served_maps[c][None, :, None, :], axis=-1).reshape(-1)
        )
    replies = jnp.concatenate([attended.reshape(local_beams, -1), jnp.stack(read_out)], axis=1)
    reply_above = lax.dynamic_index_in_dim(replies, slot_above, 0, keepdims=False)
    reply_below = lax.dynamic_index_in_dim(replies, slot_below, 0, keepdims=False)
    reply_from_below = from_behind(reply_above, "beam", 1)
    reply_from_above = from_behind(reply_below, "beam", -1)
    answer = by_origin(replies, reply_from_below, reply_from_above)
    attention_out = answer[:, :query_width].astype(jnp.bfloat16)

    inputs_x = head_input.astype(jnp.float32).reshape(local_beams, local_heads, head_dim)
    gate_values = gate_input.astype(jnp.float32).reshape(local_beams, local_heads, head_dim)
    step_size = jax.nn.softplus(step_input.astype(jnp.float32) + step_bias)
    retain = jnp.exp(-step_size * jnp.exp(decay_log))
    maps_all = state_maps.astype(jnp.float32).reshape(local_beams, 2, GROUPS, state_dim)
    drive = step_size[:, :, None] * inputs_x

    per_group = HEADS // GROUPS
    rows = local_heads // GROUPS
    overlap = jnp.sum(maps_all[:, 0] * maps_all[:, 1], axis=-1)
    overlap_heads = jnp.tile(overlap, (1, rows))
    read_back = answer[:, query_width:].reshape(local_beams, local_heads, head_dim)
    mixed_all = (
        retain[:, :, None] * read_back
        + drive * overlap_heads[:, :, None]
        + skip_gain[None, :, None] * inputs_x
    )
    gated_out = mixed_all * jax.nn.silu(gate_values)
    head_power = jnp.sum(gated_out * gated_out, axis=-1)
    partial_power = jnp.sum(head_power.reshape(local_beams, rows, GROUPS), axis=1)
    group_power = lax.psum(partial_power, "tp")
    inverse = lax.rsqrt(group_power / (per_group * head_dim) + 1e-05)
    inverse_heads = jnp.tile(inverse, (1, rows))
    mixer_out = (
        (gated_out * inverse_heads[..., None]).reshape(local_beams, local_heads * head_dim)
        * norm_gain
    ).astype(jnp.bfloat16)

    drive_columns = drive.reshape(local_beams, local_heads // block, block, head_dim).transpose(
        0, 1, 3, 2
    )
    child_state = None
    for first, (below, above) in zip(firsts, arrived):
        child_state = grow(
            relative,
            local_index,
            recurrent_state,
            below,
            above,
            drive_columns,
            retain,
            maps_all[:, 0],
            first,
            block,
            child_state,
        )
    return (child_state, mixer_out, attention_out)


def solution(mesh):
    return jax.shard_map(
        shards,
        mesh=mesh,
        in_specs=(
            P("beam", "tp"),
            P("beam", "tp"),
            P("beam", None, None),
            P("beam", "tp"),
            P("tp"),
            P("tp"),
            P("tp"),
            P("tp"),
            P("beam", "tp", None, None),
            P("beam", "tp"),
            P("beam", None, "tp"),
            P("beam", None, None, "tp"),
            P("beam", None),
            P(),
            P(),
        ),
        out_specs=(P("beam", "tp", None, None), P("beam", "tp"), P("beam", "tp")),
        check_vma=False,
    )
```

```python
import functools

import jax
import jax.numpy as jnp
from jax import lax
from jax.experimental import pallas as pl
from jax.experimental.pallas import tpu as pltpu
from jax.sharding import PartitionSpec as P


HEADS = 128
GROUPS = 4
ATT_DIM = 128
CHUNK_EIGHTHS = (2, 3, 2, 1)
VMEM_LIMIT = 24 * 2**20


def exchange(value, axis, far):
    pairs = [(one, one + 1) for one in range(far, lax.axis_size(axis) - 1, 2)]
    return lax.ppermute(value, axis, pairs + [(two, one) for one, two in pairs])


def near_way(device):
    return 1 - 2 * lax.rem(device, 2)


def origin(parents, device, child, local_beams):
    offset = parents[device * local_beams + child] - device * local_beams
    way = jnp.where(offset < 0, -1, jnp.where(offset >= local_beams, 1, 0)).astype(jnp.int32)
    return way, jnp.clip(offset - way * local_beams, 0, local_beams - 1)


def wanted_by(parents, device, way, local_beams, total_beams):
    start = jnp.clip((device + way) * local_beams, 0, total_beams - local_beams)
    index = jnp.int32(0)
    for j in range(local_beams):
        offset = parents[start + j] - device * local_beams
        index = jnp.where((offset >= 0) & (offset < local_beams), offset, index)
    return index


def full_spec(space):
    return pl.BlockSpec(memory_space=space)


SMEM, VMEM, ANY = pltpu.SMEM, pltpu.VMEM, pl.ANY


def narrow_kernel(first, block, parents, device, state, *rest):
    *asking, wide, sems = rest
    near_out, far_out = asking[-2:]
    asking = asking[:-2]
    local_beams = state.shape[0]
    total_beams = parents.shape[0]
    here = device[0]
    way = near_way(here)
    tiles = wide.shape[1] // block
    picks = [wanted_by(parents, here, w, local_beams, total_beams) for w in (way, -way)]

    def copy(side, t):
        return pltpu.make_async_copy(
            state.at[picks[side], pl.ds(first + t * block, block)],
            wide.at[side, pl.ds(t * block, block)],
            sems.at[side, t],
        )

    for t in range(tiles):
        for side in range(2):
            copy(side, t).start()
    if asking:
        ask(parents, here, way, *asking)
    for t in range(tiles):
        for side, out in enumerate((near_out, far_out)):
            copy(side, t).wait()
            rows = slice(t * block, (t + 1) * block)
            out[rows] = wide[side, rows].astype(jnp.bfloat16)


def ask(parents, here, way, queries, fresh, maps, own_ask, near_ask, far_ask, rows):
    local_beams = queries.shape[0]
    for c in range(local_beams):
        row = 0
        for source in (
            queries[c : c + 1],
            fresh[c, 0:1],
            fresh[c, 1:2],
            maps[c, 1:2],
        ):
            source = source.astype(jnp.float32)
            for k in range(source.shape[1] // ATT_DIM):
                rows[row : row + 1] = source[:, k * ATT_DIM : (k + 1) * ATT_DIM]
                row += 1
        asked = rows[...].astype(jnp.bfloat16)
        own_ask[c] = asked
        from_way, _ = origin(parents, here, c, local_beams)

        @pl.when(from_way == way)
        def _():
            near_ask[...] = asked

        @pl.when(from_way == -way)
        def _():
            far_ask[...] = asked


def narrow(state, parents, place, first, count, block, asking=()):
    local_beams, _, head_dim, state_dim = state.shape
    out = jax.ShapeDtypeStruct((count, head_dim, state_dim), jnp.bfloat16)
    out_shape = [out, out]
    scratch = [
        pltpu.VMEM((2, count, head_dim, state_dim), jnp.float32),
        pltpu.SemaphoreType.DMA((2, count // block)),
    ]
    if asking:
        queries, fresh, maps = asking
        depth = (queries.shape[1] + 2 * fresh.shape[2] + maps.shape[2]) // ATT_DIM
        message = jax.ShapeDtypeStruct((depth, ATT_DIM), jnp.bfloat16)
        own = jax.ShapeDtypeStruct((local_beams, depth, ATT_DIM), jnp.bfloat16)
        out_shape += [own, message, message]
        scratch.append(pltpu.VMEM((depth, ATT_DIM), jnp.float32))

    def kernel(parents, place, state, *rest):
        if not asking:
            return narrow_kernel(first, block, parents, place, state, *rest)
        queries, fresh, maps, near, far, own, near_ask, far_ask, wide, sems, rows = rest
        return narrow_kernel(
            first, block, parents, place, state,
            queries, fresh, maps, own, near_ask, far_ask, rows, near, far, wide, sems,
        )

    return pl.pallas_call(
        kernel,
        out_shape=tuple(out_shape),
        in_specs=[full_spec(SMEM), full_spec(SMEM), full_spec(ANY)]
        + [full_spec(VMEM)] * len(asking),
        out_specs=tuple(full_spec(VMEM) for _ in out_shape),
        scratch_shapes=scratch,
        cost_estimate=pl.CostEstimate(
            flops=0, bytes_accessed=8 * count * head_dim * state_dim, transcendentals=0
        ),
        compiler_params=pltpu.CompilerParams(vmem_limit_bytes=VMEM_LIMIT),
        name="narrow",
    )(parents, place, state, *asking)


def grow_kernel(first, block, parents, device, state, near, far, drive, retain, maps, *rest):
    out, wide, columns, in_sems, out_sems, drive_sems = rest[-6:]
    local_beams, count = wide.shape[:2]
    tiles = count // block
    base = first // block
    here = device[0]
    way = near_way(here)
    origins = [origin(parents, here, c, local_beams) for c in range(local_beams)]

    def load(c):
        _, local = origins[c]
        return pltpu.make_async_copy(
            state.at[local, pl.ds(first, count)], wide.at[c], in_sems.at[c]
        )

    def load_drive(c):
        return pltpu.make_async_copy(
            drive.at[c, pl.ds(base, tiles)], columns.at[c], drive_sems.at[c]
        )

    def store(c, t):
        return pltpu.make_async_copy(
            wide.at[c, pl.ds(t * block, block)],
            out.at[c, pl.ds(first + t * block, block)],
            out_sems.at[c, t],
        )

    for c in range(local_beams):
        load_drive(c).start()

        @pl.when(origins[c][0] == 0)
        def _():
            load(c).start()

    for c in range(local_beams):
        from_way, _ = origins[c]
        load_drive(c).wait()

        @pl.when(from_way == 0)
        def _():
            load(c).wait()

        def tile(t, carry):
            def update(previous):
                for j in range(block):
                    head = t * block + j
                    wide[c, head] = (
                        retain[c, first + head] * previous(head)
                        + columns[c, t, :, j : j + 1] * maps[c, j % GROUPS : j % GROUPS + 1]
                    )

            @pl.when(from_way == 0)
            def _():
                update(lambda head: wide[c, head])

            @pl.when(from_way == way)
            def _():
                update(lambda head: near[head].astype(jnp.float32))

            @pl.when(from_way == -way)
            def _():
                update(lambda head: far[head].astype(jnp.float32))

            store(c, t).start()
            return carry

        lax.fori_loop(0, tiles, tile, 0)
    for c in range(local_beams):
        for t in range(tiles):
            store(c, t).wait()


def grow(parents, place, state, near, far, drive, retain, maps, first, block, partial):
    local_beams, _, head_dim, state_dim = state.shape
    count = near.shape[0]
    tiles = count // block
    spaces = [SMEM, SMEM, ANY, VMEM, VMEM, ANY, SMEM, VMEM]
    operands = [parents, place, state, near, far, drive, retain, maps]
    aliases = {}
    if partial is not None:
        aliases = {len(operands): 0}
        spaces.append(ANY)
        operands.append(partial)
    return pl.pallas_call(
        functools.partial(grow_kernel, first, block),
        out_shape=jax.ShapeDtypeStruct(state.shape, jnp.float32),
        in_specs=[full_spec(space) for space in spaces],
        out_specs=full_spec(ANY),
        scratch_shapes=[
            pltpu.VMEM((local_beams, count, head_dim, state_dim), jnp.float32),
            pltpu.VMEM((local_beams, tiles, head_dim, block), jnp.float32),
            pltpu.SemaphoreType.DMA((local_beams,)),
            pltpu.SemaphoreType.DMA((local_beams, tiles)),
            pltpu.SemaphoreType.DMA((local_beams,)),
        ],
        input_output_aliases=aliases,
        cost_estimate=pl.CostEstimate(
            flops=4 * local_beams * count * head_dim * state_dim,
            bytes_accessed=6 * local_beams * count * head_dim * state_dim,
            transcendentals=0,
        ),
        compiler_params=pltpu.CompilerParams(vmem_limit_bytes=VMEM_LIMIT),
        name="grow",
    )(*operands)


def attend_kernel(
    parents, device, table, lengths, own_ask, near_ask, far_ask, pool, out, maps_out, pages, sems
):
    local_beams, page_count = table.shape
    total_beams = parents.shape[0]
    kv_heads = pool.shape[3] // ATT_DIM
    query_heads = out.shape[1]
    group = query_heads // kv_heads
    positions = page_count * pool.shape[2]
    factor = ATT_DIM ** (-0.5)
    here = device[0]
    way = near_way(here)
    near_pick = wanted_by(parents, here, way, local_beams, total_beams)
    far_pick = wanted_by(parents, here, -way, local_beams, total_beams)
    served, copies = [], []
    for c in range(local_beams):
        from_way, local = origin(parents, here, c, local_beams)
        pick = jnp.where(from_way == 0, local, jnp.where(from_way == way, near_pick, far_pick))
        served.append((from_way, pick))
        copies.append(
            [
                pltpu.make_async_copy(pool.at[table[pick, j]], pages.at[c, j], sems.at[c, j])
                for j in range(page_count)
            ]
        )
    for some in copies:
        for copy in some:
            copy.start()
    for c in range(local_beams):
        from_way, pick = served[c]
        length = lengths[here * local_beams + pick]
        asked = jnp.where(
            from_way == 0,
            own_ask[c].astype(jnp.float32),
            jnp.where(
                from_way == way, near_ask[...].astype(jnp.float32), far_ask[...].astype(jnp.float32)
            ),
        )
        keys_at = query_heads
        values_at = query_heads + kv_heads
        maps_out[c] = asked[query_heads + 2 * kv_heads :]
        for copy in copies[c]:
            copy.wait()
        for g in range(kv_heads):
            lanes = slice(g * ATT_DIM, (g + 1) * ATT_DIM)
            rows = asked[g * group : (g + 1) * group]
            keys = pages[c, :, 0, :, lanes].reshape(positions, ATT_DIM)
            values = pages[c, :, 1, :, lanes].reshape(positions, ATT_DIM)
            own_key = asked[keys_at + g : keys_at + g + 1]
            own_value = asked[values_at + g : values_at + g + 1]
            scores = (
                lax.dot_general(
                    rows.astype(jnp.bfloat16),
                    keys,
                    (((1,), (1,)), ((), ())),
                    preferred_element_type=jnp.float32,
                )
                * factor
            )
            own_score = jnp.sum(rows * own_key, axis=1, keepdims=True) * factor
            live = lax.broadcasted_iota(jnp.int32, scores.shape, 1) < length
            masked = jnp.where(live, scores, -1e30)
            highest = jnp.maximum(jnp.max(masked, axis=1, keepdims=True), own_score)
            weights = jnp.where(live, jnp.exp(masked - highest), 0.0).astype(jnp.bfloat16)
            own_weight = jnp.exp(own_score - highest).astype(jnp.bfloat16).astype(jnp.float32)
            total = jnp.sum(weights.astype(jnp.float32), axis=1, keepdims=True) + own_weight
            summed = jnp.dot(weights, values, preferred_element_type=jnp.float32)
            out[c, g * group : (g + 1) * group] = (summed + own_weight * own_value) / total


def attend(parents, place, table, lengths, own_ask, near_ask, far_ask, pool, query_heads):
    local_beams, page_count = table.shape
    kv_heads = pool.shape[3] // ATT_DIM
    map_rows = own_ask.shape[1] - query_heads - 2 * kv_heads
    positions = page_count * pool.shape[2]
    return pl.pallas_call(
        attend_kernel,
        out_shape=(
            jax.ShapeDtypeStruct((local_beams, query_heads, ATT_DIM), jnp.float32),
            jax.ShapeDtypeStruct((local_beams, map_rows, ATT_DIM), jnp.float32),
        ),
        in_specs=[full_spec(SMEM)] * 4 + [full_spec(VMEM)] * 3 + [full_spec(ANY)],
        out_specs=(full_spec(VMEM), full_spec(VMEM)),
        scratch_shapes=[
            pltpu.VMEM((local_beams, page_count) + pool.shape[1:], jnp.bfloat16),
            pltpu.SemaphoreType.DMA((local_beams, page_count)),
        ],
        cost_estimate=pl.CostEstimate(
            flops=4 * local_beams * query_heads * positions * ATT_DIM,
            bytes_accessed=4 * local_beams * positions * pool.shape[3],
            transcendentals=local_beams * query_heads * positions,
        ),
        compiler_params=pltpu.CompilerParams(vmem_limit_bytes=VMEM_LIMIT),
        name="attend",
    )(parents, place, table, lengths, own_ask, near_ask, far_ask, pool)


def chunks_of(local_heads):
    unit = local_heads // 8
    if unit % GROUPS:
        return (local_heads // 2, local_heads // 2), GROUPS
    return tuple(eighths * unit for eighths in CHUNK_EIGHTHS), unit


def shards(
    head_input,
    gate_input,
    state_maps,
    step_input,
    step_bias,
    decay_log,
    skip_gain,
    norm_gain,
    recurrent_state,
    queries,
    fresh_cache,
    cache_pool,
    page_table,
    context_length,
    parents,
):
    local_beams, local_heads, head_dim, state_dim = recurrent_state.shape
    total_beams = parents.shape[0]
    query_width = queries.shape[1]
    device = lax.axis_index("beam").astype(jnp.int32)
    place = device.reshape(1)
    sizes, block = chunks_of(local_heads)
    firsts = [sum(sizes[:k]) for k in range(len(sizes))]

    arrived = []
    for k, (first, size) in enumerate(zip(firsts, sizes)):
        asking = () if k else (queries, fresh_cache, state_maps)
        near, far, *asked = narrow(recurrent_state, parents, place, first, size, block, asking)
        near = exchange(near, "beam", 0)
        far = exchange(far, "beam", 1)
        arrived.append((near, far))
        if asked:
            own_ask, near_ask, far_ask = asked
            near_ask = exchange(near_ask, "beam", 0)
            far_ask = exchange(far_ask, "beam", 1)

    attended, served_maps = attend(
        parents,
        place,
        page_table,
        context_length,
        own_ask,
        near_ask,
        far_ask,
        cache_pool,
        query_width // ATT_DIM,
    )
    way = near_way(device)
    origins = [origin(parents, device, c, local_beams) for c in range(local_beams)]
    near_pick = wanted_by(parents, device, way, local_beams, total_beams)
    far_pick = wanted_by(parents, device, -way, local_beams, total_beams)
    served_maps = served_maps.reshape(local_beams, 1, GROUPS, 1, state_dim)
    replies = []
    for c in range(local_beams):
        from_way, local = origins[c]
        pick = jnp.where(from_way == 0, local, jnp.where(from_way == way, near_pick, far_pick))
        parent_state = lax.dynamic_index_in_dim(recurrent_state, pick, 0, keepdims=False)
        parent_state = parent_state.reshape(-1, GROUPS, head_dim, state_dim)
        read_out = jnp.sum(parent_state * served_maps[c], axis=-1)
        replies.append(jnp.concatenate([attended[c].reshape(-1), read_out.reshape(-1)]))
    near_reply, far_reply = replies[0], replies[0]
    for c in range(1, local_beams):
        near_reply = jnp.where(origins[c][0] == way, replies[c], near_reply)
        far_reply = jnp.where(origins[c][0] == -way, replies[c], far_reply)
    near_reply = exchange(near_reply, "beam", 0)
    far_reply = exchange(far_reply, "beam", 1)
    answer = jnp.stack(
        [
            jnp.where(
                from_way == 0, replies[c], jnp.where(from_way == way, near_reply, far_reply)
            )
            for c, (from_way, _) in enumerate(origins)
        ]
    )
    attention_out = answer[:, :query_width].astype(jnp.bfloat16)

    inputs_x = head_input.astype(jnp.float32).reshape(local_beams, local_heads, head_dim)
    gate_values = gate_input.astype(jnp.float32).reshape(local_beams, local_heads, head_dim)
    step_size = jax.nn.softplus(step_input.astype(jnp.float32) + step_bias)
    retain = jnp.exp(-step_size * jnp.exp(decay_log))
    maps_all = state_maps.astype(jnp.float32).reshape(local_beams, 2, GROUPS, state_dim)
    drive = step_size[:, :, None] * inputs_x

    per_group = HEADS // GROUPS
    rows = local_heads // GROUPS
    overlap = jnp.sum(maps_all[:, 0] * maps_all[:, 1], axis=-1)
    overlap_heads = jnp.tile(overlap, (1, rows))
    read_back = answer[:, query_width:].reshape(local_beams, local_heads, head_dim)
    mixed_all = (
        retain[:, :, None] * read_back
        + drive * overlap_heads[:, :, None]
        + skip_gain[None, :, None] * inputs_x
    )
    gated_out = mixed_all * jax.nn.silu(gate_values)
    head_power = jnp.sum(gated_out * gated_out, axis=-1)
    partial_power = jnp.sum(head_power.reshape(local_beams, rows, GROUPS), axis=1)
    group_power = lax.psum(partial_power, "tp")
    inverse = lax.rsqrt(group_power / (per_group * head_dim) + 1e-05)
    inverse_heads = jnp.tile(inverse, (1, rows))
    mixer_out = (
        (gated_out * inverse_heads[..., None]).reshape(local_beams, local_heads * head_dim)
        * norm_gain
    ).astype(jnp.bfloat16)

    drive_columns = drive.reshape(local_beams, local_heads // block, block, head_dim).transpose(
        0, 1, 3, 2
    )
    child_state = None
    for first, (near, far) in zip(firsts, arrived):
        child_state = grow(
            parents,
            place,
            recurrent_state,
            near,
            far,
            drive_columns,
            retain,
            maps_all[:, 0],
            first,
            block,
            child_state,
        )
    return (child_state, mixer_out, attention_out)


def solution(mesh):
    return jax.shard_map(
        shards,
        mesh=mesh,
        in_specs=(
            P("beam", "tp"),
            P("beam", "tp"),
            P("beam", None, None),
            P("beam", "tp"),
            P("tp"),
            P("tp"),
            P("tp"),
            P("tp"),
            P("beam", "tp", None, None),
            P("beam", "tp"),
            P("beam", None, "tp"),
            P("beam", None, None, "tp"),
            P("beam", None),
            P(),
            P(),
        ),
        out_specs=(P("beam", "tp", None, None), P("beam", "tp"), P("beam", "tp")),
        check_vma=False,
    )
```
